256 devices in a mesh: tm: 16 (over y, x_hi, core), col: 16 (over z, x_lo).
Axes of the slice: x: 4 (x_hi: 2, x_lo: 2; x = x_hi * 2 + x_lo), y: 4, z: 8, core: 2. Of those that a mesh axis runs over, the one named last changes fastest.
Arguments:
- occ_rows: bfloat16 [1024, 1024], P(None, 'col'), may hold values from -2.5 to 2.5
- emp_rows: bfloat16 [1024, 1024], P(None, 'col'), may hold values from -2.5 to 2.5
- occ_cols: bfloat16 [1024, 16384], P(None, 'col'), may hold values from -2.5 to 2.5
- emp_cols: bfloat16 [1024, 16384], P(None, 'col'), may hold values from -2.5 to 2.5
- occ_energy: float32 [1024], replicated, may hold values from 0.1 to 1.5
- emp_energy: float32 [1024], replicated, may hold values from 0.1 to 1.5
- time_points: float32 [16], replicated, may hold values from 0.1 to 2
- time_weights: float32 [16], replicated, may hold values from 0.1 to 1
- frequencies: float32 [16], replicated, may hold values from 0.1 to 4
- trial_vectors: float32 [16384, 512], P('col'), may hold values from -0.046875 to 0.046875
Outputs:
- response: float32 [16, 1024, 512], P('tm', 'col')
The draws below stay inside these ranges and needn't reach their ends.
All inputs are finite; a program needn't handle non-finite values.
Results may differ from the reference program's by a relative error of at most 0.0025.
Values may be sent and summed in bfloat16 or wider, within the bound.
No kernel may reach another device: no remote copies, remote signals or barrier semaphores. Data moves between devices by JAX's collectives and lax.ppermute only.
A program may use at most 64 MiB of HBM per device.

```python
import math
import jax
import jax.numpy as jnp
from jax import lax

NOCC = 1024
NEMP = 1024
NTRIAL = 512
ROWS = 1024
COLS = 16384
TIMES = 16
FREQS = 16


def block_scale(stream_key, dims, pieces, smallest, top_value):
    def one(dim, blocks):
        steps = jax.random.uniform(jax.random.fold_in(jax.random.fold_in(stream_key, 6), dim), (blocks,), jnp.float32, smallest / len(pieces), top_value / len(pieces))
        return jnp.repeat(jnp.exp(steps), dims[dim] // blocks).reshape((-1,) + (1,) * (len(dims) - dim - 1))

    loudness = one(*pieces[0])
    for cut in pieces[1:]:
        loudness = loudness * one(*cut)
    return loudness


def gaussian(stream_key, extent, width, limit, shards=(), dtype=jnp.bfloat16):
    values = jax.random.normal(stream_key, extent, jnp.float32) * width
    if len(shards) > 0:
        values = block_scale(stream_key, extent, shards, -0.22, 0.18) * values
    return jnp.clip(values, min=-limit, max=limit).astype(dtype)


def setup_inputs(seed: int = 0) -> dict:
    streams_of = jax.random.split(jax.random.key(seed), 11)
    return {
        "occ_rows": gaussian(streams_of[0], (NOCC, ROWS), (NOCC ** -0.25), 2.5, ((1, 16),)),
        "emp_rows": gaussian(streams_of[1], (NEMP, ROWS), (NEMP ** -0.25), 2.5, ((1, 16),)),
        "occ_cols": gaussian(streams_of[2], (NOCC, COLS), (NOCC ** -0.25), 2.5, ((1, 16),)),
        "emp_cols": gaussian(streams_of[3], (NEMP, COLS), (NEMP ** -0.25), 2.5, ((1, 16),)),
        "occ_energy": jnp.clip(jnp.exp(jax.random.uniform(streams_of[4], (NOCC,), jnp.float32, math.log(0.1), math.log(1.5))), 0.1, 1.5),
        "emp_energy": jnp.clip(jnp.exp(jax.random.uniform(streams_of[5], (NEMP,), jnp.float32, math.log(0.1), math.log(1.5))), 0.1, 1.5),
        "time_points": jnp.clip(jnp.exp(jax.random.uniform(streams_of[6], (TIMES,), jnp.float32, math.log(0.1), math.log(2.0))), 0.1, 2.0),
        "time_weights": jnp.clip(jnp.exp(jax.random.uniform(streams_of[7], (TIMES,), jnp.float32, math.log(0.1), math.log(1.0))), 0.1, 1.0),
        "frequencies": jnp.clip(jnp.exp(jax.random.uniform(streams_of[8], (FREQS,), jnp.float32, math.log(0.1), math.log(4.0))), 0.1, 4.0),
        "trial_vectors": gaussian(streams_of[9], (COLS, NTRIAL), COLS ** -0.5, 0.046875, ((0, 16),), jnp.float32),
    }


def scaled_states(columns, energy, moment):
    factor = jnp.exp(-energy * moment)
    return (columns.astype(jnp.float32) * factor[:, None]).astype(jnp.bfloat16)


def green_product(rows, columns):
    return lax.dot_general(rows, columns, (((0,), (0,)), ((), ())), preferred_element_type=jnp.float32)


def reference(occ_rows, emp_rows, occ_cols, emp_cols, occ_energy, emp_energy, time_points, time_weights, frequencies, trial_vectors):
    cos_table = time_weights[None, :] * jnp.cos(frequencies[:, None] * time_points[None, :])

    def one_time(moment):
        green_occ = green_product(occ_rows, scaled_states(occ_cols, occ_energy, moment))
        green_emp = green_product(emp_rows, scaled_states(emp_cols, emp_energy, moment))
        polar = green_occ * green_emp
        return jnp.dot(polar, trial_vectors, precision=lax.Precision.HIGHEST, preferred_element_type=jnp.float32)

    partial_value = lax.map(one_time, time_points)
    return jnp.einsum("kt,trj->krj", cos_table, partial_value, precision=lax.Precision.HIGHEST)
```

```python
import jax
import jax.numpy as jnp
from jax import lax
from jax.sharding import Mesh
from jax.sharding import PartitionSpec as P


def body(
    occ_rows,
    emp_rows,
    occ_cols,
    emp_cols,
    occ_energy,
    emp_energy,
    time_points,
    time_weights,
    frequencies,
    trial_vectors,
):
    teams, peers = lax.axis_size("tm"), lax.axis_size("col")
    states, rows = occ_rows.shape
    trials = trial_vectors.shape[1]
    times = time_points.shape[0]
    share = rows // teams
    team = lax.axis_index("tm")

    both = jnp.stack([occ_rows.T, emp_rows.T]).reshape(2, teams, share, states)
    mine = lax.dynamic_index_in_dim(both, team, 1, keepdims=False)
    sent = jnp.broadcast_to(mine[None], (peers, 2, share, states)).reshape(peers, 2 * share, states)
    got = lax.all_to_all(sent, "col", split_axis=0, concat_axis=0, tiled=True)
    got = got.reshape(peers, 2, share, states)

    def green(rows_in, energy, columns):
        factor = jnp.exp(-energy[None, :] * time_points[:, None])
        scaled = rows_in.astype(jnp.float32)[:, None, :, :] * factor[None, :, None, :]
        scaled = scaled.astype(jnp.bfloat16).reshape(peers * times * share, states)
        return jnp.dot(scaled, columns, preferred_element_type=jnp.float32)

    polar = green(got[:, 0], occ_energy, occ_cols) * green(got[:, 1], emp_energy, emp_cols)
    partial = jnp.dot(
        polar, trial_vectors, precision=lax.Precision.HIGH, preferred_element_type=jnp.float32
    )
    partial = partial.astype(jnp.bfloat16).reshape(peers, times * share, trials)
    arrived = lax.all_to_all(partial, "col", split_axis=0, concat_axis=0, tiled=True)
    summed = arrived.astype(jnp.float32).sum(axis=0)

    cos_table = time_weights[None, :] * jnp.cos(frequencies[:, None] * time_points[None, :])
    freqs = frequencies.shape[0]
    spread = (cos_table[:, None, :, None] * jnp.eye(share)[None, :, None, :]).reshape(
        freqs * share, times * share
    )
    spectral = jnp.dot(
        spread, summed, precision=lax.Precision.HIGHEST, preferred_element_type=jnp.float32
    )
    out = lax.all_to_all(
        spectral.reshape(freqs, share, trials), "tm", split_axis=0, concat_axis=0, tiled=True
    )
    return out.reshape(1, rows, trials)


def solution(mesh):
    in_specs = (
        P(None, "col"),
        P(None, "col"),
        P(None, "col"),
        P(None, "col"),
        P(),
        P(),
        P(),
        P(),
        P(),
        P("col", None),
    )
    out_specs = P("tm", "col", None)
    return jax.shard_map(body, mesh=mesh, in_specs=in_specs, out_specs=out_specs, check_vma=False)
```

```python
import functools

import jax
import jax.numpy as jnp
from jax import lax
from jax.experimental import pallas as pl
from jax.experimental.pallas import tpu as pltpu
from jax.sharding import Mesh
from jax.sharding import PartitionSpec as P

COL = ("z", "xl")
ALL = ("tm", "z", "xl")
F32, BF16 = jnp.float32, jnp.bfloat16
SMALL, LARGE = 12 << 20, 28 << 20


def pick_kernel(share, shares_ref, occ_ref, emp_ref, out_ref):
    rows = occ_ref.shape[0]
    line = lax.broadcasted_iota(jnp.int32, (2 * share, rows), 0)
    point = lax.broadcasted_iota(jnp.int32, (2 * share, rows), 1)
    for side in range(2):
        first = shares_ref[side] * share
        occ_pick = jnp.where((line < share) & (point == first + line), 1.0, 0.0).astype(BF16)
        emp_pick = jnp.where((line >= share) & (point == first + line - share), 1.0, 0.0)
        both = jnp.dot(occ_pick, occ_ref[...], preferred_element_type=F32)
        both += jnp.dot(emp_pick.astype(BF16), emp_ref[...], preferred_element_type=F32)
        both = both.astype(BF16)
        for peer in range(side, out_ref.shape[0], 2):
            out_ref[peer] = both


def pick(shares, occ_t, emp_t, peers, share):
    states = occ_t.shape[1]
    return pl.pallas_call(
        functools.partial(pick_kernel, share),
        out_shape=jax.ShapeDtypeStruct((peers, 2 * share, states), BF16),
        in_specs=[
            pl.BlockSpec(memory_space=pltpu.SMEM),
            pl.BlockSpec(memory_space=pltpu.VMEM),
            pl.BlockSpec(memory_space=pltpu.VMEM),
        ],
        out_specs=pl.BlockSpec(memory_space=pltpu.VMEM),
        compiler_params=pltpu.CompilerParams(vmem_limit_bytes=SMALL),
    )(shares, occ_t, emp_t)


def prepare_kernel(times_ref, energy_ref, trial_ref, factor_ref, high_ref, low_ref):
    for kind in range(2):
        factor_ref[kind] = jnp.exp(-energy_ref[kind : kind + 1, :] * times_ref[...])
    for start in range(0, trial_ref.shape[0], 256):
        value = trial_ref[start : start + 256, :]
        high = value.astype(BF16)
        high_ref[start : start + 256, :] = high
        low_ref[start : start + 256, :] = (value - high.astype(F32)).astype(BF16)


def prepare(times, energy, trial):
    states = energy.shape[1]
    return pl.pallas_call(
        prepare_kernel,
        out_shape=(
            jax.ShapeDtypeStruct((2, times.shape[0], states), F32),
            jax.ShapeDtypeStruct(trial.shape, BF16),
            jax.ShapeDtypeStruct(trial.shape, BF16),
        ),
        in_specs=[pl.BlockSpec(memory_space=pltpu.VMEM)] * 3,
        out_specs=(pl.BlockSpec(memory_space=pltpu.VMEM),) * 3,
        compiler_params=pltpu.CompilerParams(vmem_limit_bytes=SMALL),
    )(times, energy, trial)


def product_kernel(
    share, xl_ref, rows_ref, factor_ref, occ_ref, emp_ref, high_ref, low_ref, out_ref, occ_s, emp_s
):
    times = factor_ref.shape[1]
    block = pl.program_id(0)
    per_step = occ_s.shape[0] // (share * times)
    for index in range(per_step):
        peer = 2 * (block * per_step + index) + xl_ref[0]
        rows = rows_ref[peer].astype(F32)
        for r in range(share):
            at = (index * share + r) * times
            occ_s[at : at + times, :] = (rows[r : r + 1, :] * factor_ref[0]).astype(BF16)
            emp_s[at : at + times, :] = (
                rows[share + r : share + r + 1, :] * factor_ref[1]
            ).astype(BF16)
    polar = jnp.dot(occ_s[...], occ_ref[...], preferred_element_type=F32)
    polar *= jnp.dot(emp_s[...], emp_ref[...], preferred_element_type=F32)
    polar = polar.astype(BF16)
    total = jnp.dot(polar, high_ref[...], preferred_element_type=F32)
    total += jnp.dot(polar, low_ref[...], preferred_element_type=F32)
    out_ref[...] = total.astype(out_ref.dtype)


def products(xl, rows, factor, occ_cols, emp_cols, high, low, share, dtype):
    zs = rows.shape[0] // 2
    times, states = factor.shape[1:]
    trials = high.shape[1]
    per_step = 4
    lines = per_step * share * times
    whole = pl.BlockSpec(memory_space=pltpu.VMEM)
    columns = occ_cols.shape[1]
    flops = 2 * zs * share * times * columns * (2 * states + 2 * trials)
    return pl.pallas_call(
        functools.partial(product_kernel, share),
        grid=(zs // per_step,),
        out_shape=jax.ShapeDtypeStruct((zs * share * times, trials), dtype),
        in_specs=[pl.BlockSpec(memory_space=pltpu.SMEM)] + [whole] * 6,
        out_specs=pl.BlockSpec((lines, trials), lambda i: (i, 0)),
        scratch_shapes=[pltpu.VMEM((lines, states), BF16), pltpu.VMEM((lines, states), BF16)],
        compiler_params=pltpu.CompilerParams(vmem_limit_bytes=LARGE),
        cost_estimate=pl.CostEstimate(flops=flops, bytes_accessed=8 << 20, transcendentals=0),
    )(xl, rows, factor, occ_cols, emp_cols, high, low)


def x_pairs(zs):
    pairs = []
    for tm in range(16):
        for z in range(zs):
            for xl in range(2):
                other = tm ^ 2 if tm & 1 else tm
                pairs.append(((tm * zs + z) * 2 + xl, (other * zs + z) * 2 + 1 - xl))
    return pairs


def body(
    occ_rows,
    emp_rows,
    occ_cols,
    emp_cols,
    occ_energy,
    emp_energy,
    time_points,
    time_weights,
    frequencies,
    trial_vectors,
):
    teams, zs = lax.axis_size("tm"), lax.axis_size("z")
    peers = 2 * zs
    states, rows = occ_rows.shape
    trials = trial_vectors.shape[1]
    times = time_points.shape[0]
    freqs = frequencies.shape[0]
    share = rows // teams
    team, xl = lax.axis_index("tm"), lax.axis_index("xl")
    swapped = jnp.where(team & 1 == 1, team ^ 2, team)

    sent = pick(jnp.stack([team, swapped]), occ_rows.T, emp_rows.T, peers, share)
    got = lax.all_to_all(sent, COL, split_axis=0, concat_axis=0, tiled=True)

    energy = jnp.stack([occ_energy, emp_energy])
    factor, high, low = prepare(time_points[:, None], energy, trial_vectors)
    other = products(
        (1 - xl)[None], got, factor, occ_cols, emp_cols, high, low, share, BF16
    )
    arrived = lax.ppermute(other, ALL, x_pairs(zs))
    own = products(xl[None], got, factor, occ_cols, emp_cols, high, low, share, F32)
    pair = (own + arrived.astype(F32)).astype(BF16).reshape(zs, share * times, trials)
    summed = lax.all_to_all(pair, "z", split_axis=0, concat_axis=0, tiled=True)
    summed = summed.astype(F32).sum(axis=0)

    cos_table = time_weights[None, :] * jnp.cos(frequencies[:, None] * time_points[None, :])
    spread = (jnp.eye(share)[None, :, :, None] * cos_table[:, None, None, :]).reshape(
        freqs * share, share * times
    )
    spectral = jnp.dot(spread, summed, precision=lax.Precision.HIGHEST, preferred_element_type=F32)
    out = lax.all_to_all(
        spectral.reshape(freqs, share, trials), "tm", split_axis=0, concat_axis=0, tiled=True
    )
    by_share = out.reshape(teams // 4, 2, 2, share, trials)
    turned = jnp.stack([by_share[:, :, 0], by_share[:, ::-1, 1]], axis=2)
    out = jnp.where(xl == 1, turned, by_share)
    return out.reshape(1, rows, trials)


def solution(mesh):
    torus = Mesh(mesh.devices.reshape(mesh.shape["tm"], mesh.shape["col"] // 2, 2), ALL)
    in_specs = (
        P(None, COL),
        P(None, COL),
        P(None, COL),
        P(None, COL),
        P(),
        P(),
        P(),
        P(),
        P(),
        P(COL, None),
    )
    out_specs = P("tm", COL, None)
    return jax.shard_map(body, mesh=torus, in_specs=in_specs, out_specs=out_specs, check_vma=False)
```

```python
import functools

import jax
import jax.numpy as jnp
from jax import lax
from jax.experimental import pallas as pl
from jax.experimental.pallas import tpu as pltpu
from jax.sharding import Mesh
from jax.sharding import PartitionSpec as P

COL = ("z", "xl")
ALL = ("tm", "z", "xl")
F32, BF16 = jnp.float32, jnp.bfloat16
SMALL, LARGE = 12 << 20, 20 << 20
BLOCK = 4


def far_ref(value):
    return pltpu.with_memory_space_constraint(value, pltpu.HBM)


def pick_kernel(share, shares_ref, occ_ref, emp_ref, out_ref, held, sems):
    copies = []
    for side in range(2):
        near = pl.multiple_of(shares_ref[side] * share // 8 * 8, 8)
        for kind, ref in enumerate((occ_ref, emp_ref)):
            copies.append(
                pltpu.make_async_copy(
                    ref.at[pl.ds(near, 8)], held.at[2 * side + kind], sems.at[2 * side + kind]
                )
            )
    for copy in copies:
        copy.start()
    line = lax.broadcasted_iota(jnp.int32, (2 * share, 8), 0)
    point = lax.broadcasted_iota(jnp.int32, (2 * share, 8), 1)
    for side in range(2):
        first = lax.rem(shares_ref[side] * share, 8)
        occ_pick = jnp.where((line < share) & (point == first + line), 1.0, 0.0).astype(BF16)
        emp_pick = jnp.where((line >= share) & (point == first + line - share), 1.0, 0.0)
        copies[2 * side].wait()
        copies[2 * side + 1].wait()
        both = jnp.dot(occ_pick, held[2 * side], preferred_element_type=F32)
        both += jnp.dot(emp_pick.astype(BF16), held[2 * side + 1], preferred_element_type=F32)
        both = both.astype(BF16)
        for peer in range(side, out_ref.shape[0], 2):
            out_ref[peer] = both


def pick(shares, occ_t, emp_t, peers, share):
    states = occ_t.shape[1]
    return pl.pallas_call(
        functools.partial(pick_kernel, share),
        out_shape=jax.ShapeDtypeStruct((peers, 2 * share, states), BF16),
        in_specs=[
            pl.BlockSpec(memory_space=pltpu.SMEM),
            pl.BlockSpec(memory_space=pltpu.HBM),
            pl.BlockSpec(memory_space=pltpu.HBM),
        ],
        out_specs=pl.BlockSpec(memory_space=pltpu.VMEM),
        scratch_shapes=[pltpu.VMEM((4, 8, states), BF16), pltpu.SemaphoreType.DMA((4,))],
        compiler_params=pltpu.CompilerParams(vmem_limit_bytes=SMALL),
    )(shares, far_ref(occ_t), far_ref(emp_t))


def halves(value):
    high = value.astype(BF16)
    return high, (value - high.astype(F32)).astype(BF16)


def prepare_kernel(
    times_ref,
    weights_ref,
    freqs_ref,
    occ_energy_ref,
    emp_energy_ref,
    trial_ref,
    factor_ref,
    high_ref,
    low_hbm,
    spread_ref,
    low_ref,
    sem,
):
    for start in range(0, trial_ref.shape[0], 256):
        at = slice(start, start + 256)
        high_ref[at, :], low_ref[at, :] = halves(trial_ref[at, :])
    copy = pltpu.make_async_copy(low_ref, low_hbm, sem)
    copy.start()
    times, freqs = times_ref.shape[0], freqs_ref.shape[0]
    for kind, ref in enumerate((occ_energy_ref, emp_energy_ref)):
        for t in range(times):
            factor_ref[kind, t : t + 1, :] = jnp.exp(-ref[...] * times_ref[t])
    lines = spread_ref.shape[1]
    points = lines // times
    line = lax.broadcasted_iota(jnp.int32, (freqs, lines), 0)
    lane = lax.broadcasted_iota(jnp.int32, (freqs, lines), 1)
    moment, weight, freq = (jnp.zeros((freqs, lines), F32) for _ in range(3))
    for t in range(times):
        moment = jnp.where(lane % times == t, times_ref[t], moment)
        weight = jnp.where(lane % times == t, weights_ref[t], weight)
    for k in range(freqs):
        freq = jnp.where(line == k, freqs_ref[k], freq)
    table = weight * jnp.cos(freq * moment)
    point = lax.broadcasted_iota(jnp.int32, (points, lines), 0)
    same = lax.broadcasted_iota(jnp.int32, (points, lines), 1) // times == point
    for k in range(freqs):
        main, rest = halves(jnp.where(same, table[k : k + 1, :], 0.0))
        spread_ref[0, k * points : (k + 1) * points, :] = main
        spread_ref[1, k * points : (k + 1) * points, :] = rest
    copy.wait()


def prepare(times, weights, freqs, occ_energy, emp_energy, trial, points):
    states = occ_energy.shape[0]
    few = pl.BlockSpec(memory_space=pltpu.SMEM)
    whole = pl.BlockSpec(memory_space=pltpu.VMEM)
    return pl.pallas_call(
        prepare_kernel,
        out_shape=(
            jax.ShapeDtypeStruct((2, times.shape[0], states), F32),
            jax.ShapeDtypeStruct(trial.shape, BF16),
            jax.ShapeDtypeStruct(trial.shape, BF16),
            jax.ShapeDtypeStruct((2, freqs.shape[0] * points, points * times.shape[0]), BF16),
        ),
        in_specs=[few, few, few, whole, whole, whole],
        out_specs=(whole, whole, pl.BlockSpec(memory_space=pltpu.HBM), whole),
        scratch_shapes=[pltpu.VMEM(trial.shape, BF16), pltpu.SemaphoreType.DMA],
        compiler_params=pltpu.CompilerParams(vmem_limit_bytes=SMALL),
    )(*map(far_ref, (times, weights, freqs, occ_energy[None, :], emp_energy[None, :], trial)))


def product_kernel(
    share,
    first,
    xl_ref,
    rows_ref,
    factor_ref,
    occ_ref,
    emp_hbm,
    high_ref,
    low_hbm,
    out_ref,
    occ_s,
    emp_s,
    emp_ref,
    low_ref,
    sems,
):
    times = factor_ref.shape[1]
    step = pl.program_id(0)
    emp_copy = pltpu.make_async_copy(emp_hbm, emp_ref, sems.at[0])
    low_copy = pltpu.make_async_copy(low_hbm, low_ref, sems.at[1])

    @pl.when(step == 0)
    def _():
        emp_copy.start()
        low_copy.start()

    for index in range(BLOCK):
        peer = 2 * (first + step * BLOCK + index) + xl_ref[0]
        rows = rows_ref[peer].astype(F32)
        for r in range(share):
            at = (index * share + r) * times
            occ_s[at : at + times, :] = (rows[r : r + 1, :] * factor_ref[0]).astype(BF16)
            emp_s[at : at + times, :] = (
                rows[share + r : share + r + 1, :] * factor_ref[1]
            ).astype(BF16)
    polar = jnp.dot(occ_s[...], occ_ref[...], preferred_element_type=F32)

    @pl.when(step == 0)
    def _():
        emp_copy.wait()

    polar *= jnp.dot(emp_s[...], emp_ref[...], preferred_element_type=F32)
    polar = polar.astype(BF16)

    @pl.when(step == 0)
    def _():
        low_copy.wait()

    total = jnp.dot(polar, high_ref[...], preferred_element_type=F32)
    total += jnp.dot(polar, low_ref[...], preferred_element_type=F32)
    out_ref[...] = total.astype(out_ref.dtype)


def products(xl, rows, factor, occ_cols, emp_cols, high, low, share, first, count, dtype):
    times, states = factor.shape[1:]
    columns, trials = high.shape
    lines = BLOCK * share * times
    whole = pl.BlockSpec(memory_space=pltpu.VMEM)
    far = pl.BlockSpec(memory_space=pltpu.HBM)
    flops = 2 * count * share * times * columns * (2 * states + 2 * trials)
    return pl.pallas_call(
        functools.partial(product_kernel, share, first),
        grid=(count // BLOCK,),
        out_shape=jax.ShapeDtypeStruct((count * share * times, trials), dtype),
        in_specs=[
            pl.BlockSpec(memory_space=pltpu.SMEM),
            whole,
            whole,
            whole,
            far,
            whole,
            far,
        ],
        out_specs=pl.BlockSpec((lines, trials), lambda i: (i, 0)),
        scratch_shapes=[
            pltpu.VMEM((lines, states), BF16),
            pltpu.VMEM((lines, states), BF16),
            pltpu.VMEM(emp_cols.shape, BF16),
            pltpu.VMEM(low.shape, BF16),
            pltpu.SemaphoreType.DMA((2,)),
        ],
        compiler_params=pltpu.CompilerParams(vmem_limit_bytes=LARGE),
        cost_estimate=pl.CostEstimate(flops=flops, bytes_accessed=8 << 20, transcendentals=0),
    )(xl, rows, factor, occ_cols, far_ref(emp_cols), high, far_ref(low))


def mix_kernel(share, own_ref, low_half_ref, high_half_ref, spread_ref, out_ref):
    spread, spread_rest = spread_ref[0], spread_ref[1]
    lines = spread_ref.shape[1]
    freqs = lines // (BLOCK * share)
    zs = out_ref.shape[0] // freqs
    for step, part_ref in enumerate((low_half_ref, high_half_ref)):
        total = own_ref[step * lines : (step + 1) * lines, :] + part_ref[...].astype(F32)
        main, rest = halves(total)
        mixed = jnp.dot(spread, rest, preferred_element_type=F32)
        mixed += jnp.dot(spread_rest, main, preferred_element_type=F32)
        mixed += jnp.dot(spread, main, preferred_element_type=F32)
        mixed = mixed.astype(BF16)
        for k in range(freqs):
            for index in range(BLOCK):
                at = (k * BLOCK + index) * share
                out_ref[k * zs + step * BLOCK + index] = mixed[at : at + share, :]


def mix(own, low_half, high_half, spread, share):
    lines, trials = own.shape
    return pl.pallas_call(
        functools.partial(mix_kernel, share),
        out_shape=jax.ShapeDtypeStruct((lines // share, share, trials), BF16),
        in_specs=[pl.BlockSpec(memory_space=pltpu.VMEM)] * 4,
        out_specs=pl.BlockSpec(memory_space=pltpu.VMEM),
        compiler_params=pltpu.CompilerParams(vmem_limit_bytes=SMALL),
    )(own, low_half, high_half, spread)


def collect_kernel(turn_ref, got_ref, out_ref):
    teams, share = out_ref.shape[:2]
    zs = got_ref.shape[0] // teams
    for place in range(teams):
        source = place ^ turn_ref[0] if place & 1 else place
        total = got_ref[source * zs].astype(F32)
        for z in range(1, zs):
            total += got_ref[source * zs + z].astype(F32)
        out_ref[place] = total


def collect(turn, got, teams):
    share, trials = got.shape[1:]
    return pl.pallas_call(
        collect_kernel,
        out_shape=jax.ShapeDtypeStruct((teams, share, trials), F32),
        in_specs=[
            pl.BlockSpec(memory_space=pltpu.SMEM),
            pl.BlockSpec(memory_space=pltpu.VMEM),
        ],
        out_specs=pl.BlockSpec(memory_space=pltpu.VMEM),
        compiler_params=pltpu.CompilerParams(vmem_limit_bytes=SMALL),
    )(turn, got)


def x_pairs(zs):
    pairs = []
    for tm in range(16):
        for z in range(zs):
            for xl in range(2):
                other = tm ^ 2 if tm & 1 else tm
                pairs.append(((tm * zs + z) * 2 + xl, (other * zs + z) * 2 + 1 - xl))
    return pairs


def body(
    occ_rows,
    emp_rows,
    occ_cols,
    emp_cols,
    occ_energy,
    emp_energy,
    time_points,
    time_weights,
    frequencies,
    trial_vectors,
):
    teams, zs = lax.axis_size("tm"), lax.axis_size("z")
    peers = 2 * zs
    states, rows = occ_rows.shape
    trials = trial_vectors.shape[1]
    share = rows // teams
    team, xl = lax.axis_index("tm"), lax.axis_index("xl")
    swapped = jnp.where(team & 1 == 1, team ^ 2, team)

    sent = pick(jnp.stack([team, swapped]), occ_rows.T, emp_rows.T, peers, share)
    got = lax.all_to_all(sent, COL, split_axis=0, concat_axis=0, tiled=True)

    factor, high, low, spread = prepare(
        time_points, time_weights, frequencies, occ_energy, emp_energy, trial_vectors, BLOCK * share
    )

    def part(side, first, count, dtype):
        return products(
            side[None], got, factor, occ_cols, emp_cols, high, low, share, first, count, dtype
        )

    pairs = x_pairs(zs)
    low_half = lax.ppermute(part(1 - xl, 0, BLOCK, BF16), ALL, pairs)
    high_half = lax.ppermute(part(1 - xl, BLOCK, BLOCK, BF16), ALL, pairs)
    own = part(xl, 0, zs, F32)
    sent = mix(own, low_half, high_half, spread, share)
    got = lax.all_to_all(sent, ("tm", "z"), split_axis=0, concat_axis=0, tiled=True)
    out = collect((2 * xl)[None], got, teams)
    return out.reshape(1, rows, trials)


def solution(mesh):
    torus = Mesh(mesh.devices.reshape(mesh.shape["tm"], mesh.shape["col"] // 2, 2), ALL)
    in_specs = (
        P(None, COL),
        P(None, COL),
        P(None, COL),
        P(None, COL),
        P(),
        P(),
        P(),
        P(),
        P(),
        P(COL, None),
    )
    out_specs = P("tm", COL, None)
    return jax.shard_map(body, mesh=torus, in_specs=in_specs, out_specs=out_specs, check_vma=False)
```

```python
import functools

import jax
import jax.numpy as jnp
from jax import lax
from jax.experimental import pallas as pl
from jax.experimental.pallas import tpu as pltpu
from jax.sharding import Mesh
from jax.sharding import PartitionSpec as P

COL = ("zh", "zl", "xl")
ALL = ("tm",) + COL
F32, BF16 = jnp.float32, jnp.bfloat16
FEW = pl.BlockSpec(memory_space=pltpu.SMEM)
WHOLE = pl.BlockSpec(memory_space=pltpu.VMEM)
SMALL, LARGE = 12 << 20, 20 << 20
BLOCK = 4
PICKCOST = 1 << 35


def far_ref(value):
    return pltpu.with_memory_space_constraint(value, pltpu.HBM)


def pick_kernel(
    share,
    times_hbm,
    occ_energy_hbm,
    emp_energy_hbm,
    occ_hbm,
    emp_hbm,
    out_ref,
    factor_ref,
    held,
    times_ref,
    energy_ref,
    sems,
):
    team = lax.axis_index("tm")
    shares = team, jnp.where(team & 1 == 1, team ^ 2, team)
    pairs = []
    for side in range(2):
        near = pl.multiple_of(shares[side] * share // 8 * 8, 8)
        for kind, ref in enumerate((occ_hbm, emp_hbm)):
            pairs.append((ref.at[pl.ds(near, 8)], held.at[2 * side + kind]))
    pairs.append((times_hbm, times_ref))
    pairs.append((occ_energy_hbm, energy_ref.at[0]))
    pairs.append((emp_energy_hbm, energy_ref.at[1]))
    copies = [pltpu.make_async_copy(*pair, sems.at[i]) for i, pair in enumerate(pairs)]
    for copy in copies:
        copy.start()
    line = lax.broadcasted_iota(jnp.int32, (2 * share, 8), 0)
    point = lax.broadcasted_iota(jnp.int32, (2 * share, 8), 1)
    for side in range(2):
        first = lax.rem(shares[side] * share, 8)
        occ_pick = jnp.where((line < share) & (point == first + line), 1.0, 0.0).astype(BF16)
        emp_pick = jnp.where((line >= share) & (point == first + line - share), 1.0, 0.0)
        copies[2 * side].wait()
        copies[2 * side + 1].wait()
        both = jnp.dot(occ_pick, held[2 * side], preferred_element_type=F32)
        both += jnp.dot(emp_pick.astype(BF16), held[2 * side + 1], preferred_element_type=F32)
        both = both.astype(BF16)
        for peer in range(side, out_ref.shape[0], 2):
            out_ref[peer] = both
    for copy in copies[4:7]:
        copy.wait()
    times = times_ref.shape[1]
    row = lax.broadcasted_iota(jnp.int32, (times, times), 0)
    lane = lax.broadcasted_iota(jnp.int32, (times, times), 1)
    moments = jnp.sum(jnp.where(row == lane, times_ref[...], 0.0), axis=1, keepdims=True)
    for kind in range(2):
        factor_ref[kind] = jnp.exp(-energy_ref[kind] * moments)


def pick(times, occ_energy, emp_energy, occ_t, emp_t, peers, share):
    states = occ_t.shape[1]
    far = pl.BlockSpec(memory_space=pltpu.HBM)
    count = times.shape[0]
    return pl.pallas_call(
        functools.partial(pick_kernel, share),
        out_shape=(
            jax.ShapeDtypeStruct((peers, 2 * share, states), BF16),
            jax.ShapeDtypeStruct((2, count, states), F32),
        ),
        in_specs=[far] * 5,
        out_specs=(WHOLE,) * 2,
        scratch_shapes=[
            pltpu.VMEM((4, 8, states), BF16),
            pltpu.VMEM((1, count), F32),
            pltpu.VMEM((2, 1, states), F32),
            pltpu.SemaphoreType.DMA((7,)),
        ],
        compiler_params=pltpu.CompilerParams(vmem_limit_bytes=SMALL),
        cost_estimate=pl.CostEstimate(flops=PICKCOST, bytes_accessed=1 << 20, transcendentals=0),
    )(
        far_ref(times[None, :]),
        far_ref(occ_energy[None, :]),
        far_ref(emp_energy[None, :]),
        far_ref(occ_t),
        far_ref(emp_t),
    )


def halves(value):
    high = value.astype(BF16)
    return high, (value - high.astype(F32)).astype(BF16)


def scale(share, part, rows_ref, factor_ref, scaled):
    times = factor_ref.shape[1]
    occ_s, emp_s = scaled
    start = 2 * (lax.axis_index("zl") ^ (part >> 1)) + (lax.axis_index("xl") ^ (part & 1))
    for index in range(BLOCK):
        rows = rows_ref[4 * index + start].astype(F32)
        for r in range(share):
            at = (index * share + r) * times
            occ_s[at : at + times, :] = (rows[r : r + 1, :] * factor_ref[0]).astype(BF16)
            emp_s[at : at + times, :] = (
                rows[share + r : share + r + 1, :] * factor_ref[1]
            ).astype(BF16)


def first_kernel(
    share,
    part,
    rows_ref,
    factor_ref,
    occ_ref,
    emp_ref,
    trial_ref,
    out_ref,
    high_ref,
    low_ref,
    *scaled,
):
    for begin in range(0, trial_ref.shape[0], 256):
        at = slice(begin, begin + 256)
        high_ref[at, :], low_ref[at, :] = halves(trial_ref[at, :])
    next_kernel(
        share, part, rows_ref, factor_ref, occ_ref, emp_ref, high_ref, low_ref, out_ref, *scaled
    )


def next_kernel(
    share, part, rows_ref, factor_ref, occ_ref, emp_ref, high_ref, low_ref, out_ref, *scaled
):
    scale(share, part, rows_ref, factor_ref, scaled)
    polar = jnp.dot(scaled[0][...], occ_ref[...], preferred_element_type=F32)
    polar *= jnp.dot(scaled[1][...], emp_ref[...], preferred_element_type=F32)
    polar = polar.astype(BF16)
    total = jnp.dot(polar, high_ref[...], preferred_element_type=F32)
    total += jnp.dot(polar, low_ref[...], preferred_element_type=F32)
    out_ref[...] = total.astype(out_ref.dtype)


def table_kernel(share, part, times_ref, weights_ref, freqs_ref, *refs):
    times, freqs = times_ref.shape[0], freqs_ref.shape[0]
    points = BLOCK * share
    lines = points * times
    line = lax.broadcasted_iota(jnp.int32, (freqs, lines), 0)
    lane = lax.broadcasted_iota(jnp.int32, (freqs, lines), 1)
    moment, weight, freq = (jnp.zeros((freqs, lines), F32) for _ in range(3))
    for t in range(times):
        moment = jnp.where(lane % times == t, times_ref[t], moment)
        weight = jnp.where(lane % times == t, weights_ref[t], weight)
    for k in range(freqs):
        freq = jnp.where(line == k, freqs_ref[k], freq)
    table = weight * jnp.cos(freq * moment)
    point = lax.broadcasted_iota(jnp.int32, (points, lines), 0)
    same = lax.broadcasted_iota(jnp.int32, (points, lines), 1) // times == point
    *inputs, out_ref, spread_ref, occ_s, emp_s = refs
    for k in range(freqs):
        main, rest = halves(jnp.where(same, table[k : k + 1, :], 0.0))
        spread_ref[0, k * points : (k + 1) * points, :] = main
        spread_ref[1, k * points : (k + 1) * points, :] = rest
    next_kernel(share, part, *inputs, out_ref, occ_s, emp_s)


def cost(lines, states, columns, trials):
    return pl.CostEstimate(
        flops=4 * lines * columns * (states + trials), bytes_accessed=8 << 20, transcendentals=0
    )


def first_products(part, rows, factor, occ_cols, emp_cols, trial, share):
    states, columns = occ_cols.shape
    lines, trials = BLOCK * share * factor.shape[1], trial.shape[1]
    return pl.pallas_call(
        functools.partial(first_kernel, share, part),
        out_shape=(
            jax.ShapeDtypeStruct((lines, trials), BF16),
            jax.ShapeDtypeStruct(trial.shape, BF16),
            jax.ShapeDtypeStruct(trial.shape, BF16),
        ),
        in_specs=[WHOLE] * 5,
        out_specs=(WHOLE,) * 3,
        scratch_shapes=[pltpu.VMEM((lines, states), BF16)] * 2,
        compiler_params=pltpu.CompilerParams(vmem_limit_bytes=LARGE),
        cost_estimate=cost(lines, states, columns, trials),
    )(rows, factor, occ_cols, emp_cols, trial)


def next_products(part, rows, factor, occ_cols, emp_cols, high, low, share, dtype, grid=None):
    times, states = factor.shape[1:]
    columns, trials = high.shape
    lines = BLOCK * share * times
    out = jax.ShapeDtypeStruct((lines, trials), dtype)
    grid = () if grid is None else grid
    return pl.pallas_call(
        functools.partial(table_kernel if grid else next_kernel, share, part),
        out_shape=(out, jax.ShapeDtypeStruct((2, lines, lines), BF16)) if grid else out,
        in_specs=[FEW] * len(grid) + [WHOLE] * 6,
        out_specs=(WHOLE, WHOLE) if grid else WHOLE,
        scratch_shapes=[pltpu.VMEM((lines, states), BF16)] * 2,
        compiler_params=pltpu.CompilerParams(vmem_limit_bytes=LARGE),
        cost_estimate=cost(lines, states, columns, trials),
    )(*grid, rows, factor, occ_cols, emp_cols, high, low)


def mix_kernel(share, spread_ref, own_ref, x_ref, z_ref, out_ref):
    total = own_ref[...] + x_ref[...].astype(F32) + z_ref[...].astype(F32)
    main, rest = halves(total)
    mixed = jnp.dot(spread_ref[0], rest, preferred_element_type=F32)
    mixed += jnp.dot(spread_ref[1], main, preferred_element_type=F32)
    mixed += jnp.dot(spread_ref[0], main, preferred_element_type=F32)
    mixed = mixed.astype(BF16)
    for place in range(out_ref.shape[0]):
        out_ref[place] = mixed[place * share : (place + 1) * share, :]


def mix(spread, own, from_x, from_z, share):
    lines, trials = own.shape
    return pl.pallas_call(
        functools.partial(mix_kernel, share),
        out_shape=jax.ShapeDtypeStruct((lines // share, share, trials), BF16),
        in_specs=[WHOLE] * 4,
        out_specs=WHOLE,
        compiler_params=pltpu.CompilerParams(vmem_limit_bytes=SMALL),
    )(spread, own, from_x, from_z)


def collect_kernel(teams, got_ref, out_ref):
    share = got_ref.shape[1]
    zs = got_ref.shape[0] // teams
    turn = 2 * lax.axis_index("xl")
    for place in range(teams):
        source = place ^ turn if place & 1 else place
        total = got_ref[source * zs].astype(F32)
        for z in range(1, zs):
            total += got_ref[source * zs + z].astype(F32)
        out_ref[0, place * share : (place + 1) * share, :] = total


def collect(got, teams):
    share, trials = got.shape[1:]
    return pl.pallas_call(
        functools.partial(collect_kernel, teams),
        out_shape=jax.ShapeDtypeStruct((1, teams * share, trials), F32),
        in_specs=[WHOLE],
        out_specs=WHOLE,
        compiler_params=pltpu.CompilerParams(vmem_limit_bytes=SMALL),
    )(got)


def pairs_of(teams, zs, along_x):
    pairs = []
    for tm in range(teams):
        for z in range(zs):
            for xl in range(2):
                if along_x:
                    to = tm ^ 2 if tm & 1 else tm, z, 1 - xl
                else:
                    to = tm, ((z - 1 + 2 * (z & 1)) % zs if tm & 1 else z ^ 1), xl
                pairs.append(((tm * zs + z) * 2 + xl, (to[0] * zs + to[1]) * 2 + to[2]))
    return pairs


def body(
    occ_rows,
    emp_rows,
    occ_cols,
    emp_cols,
    occ_energy,
    emp_energy,
    time_points,
    time_weights,
    frequencies,
    trial_vectors,
):
    teams, zs = lax.axis_size("tm"), 2 * lax.axis_size("zh")
    share = occ_rows.shape[1] // teams

    sent, factor = pick(
        time_points,
        occ_energy,
        emp_energy,
        occ_rows.T,
        emp_rows.T,
        2 * zs,
        share,
    )
    rows = lax.all_to_all(sent, COL, split_axis=0, concat_axis=0, tiled=True)

    x_pairs, z_pairs = pairs_of(teams, zs, True), pairs_of(teams, zs, False)
    with jax.named_scope("for_both"):
        both, high, low = first_products(
            3, rows, factor, occ_cols, emp_cols, trial_vectors, share
        )
    held = (rows, factor, occ_cols, emp_cols, high, low, share)
    with jax.named_scope("x_first"):
        from_x = lax.ppermute(both, ALL, x_pairs)
    with jax.named_scope("for_x"):
        along_x = next_products(1, *held, BF16)
    with jax.named_scope("x_second"):
        own_from_x = lax.ppermute(along_x, ALL, x_pairs)
    with jax.named_scope("for_z"):
        along_z = next_products(2, *held, F32)
    with jax.named_scope("z_only"):
        from_z = lax.ppermute((along_z + from_x.astype(F32)).astype(BF16), ALL, z_pairs)
    with jax.named_scope("for_own"):
        grid = tuple(map(far_ref, (time_points, time_weights, frequencies)))
        own, spread = next_products(0, *held, F32, grid)
    sent = mix(spread, own, own_from_x, from_z, share)
    got = lax.all_to_all(sent, ("tm", "zh"), split_axis=0, concat_axis=0, tiled=True)
    return collect(got, teams)


def solution(mesh):
    torus = Mesh(mesh.devices.reshape(mesh.shape["tm"], mesh.shape["col"] // 4, 2, 2), ALL)
    in_specs = (
        P(None, COL),
        P(None, COL),
        P(None, COL),
        P(None, COL),
        P(),
        P(),
        P(),
        P(),
        P(),
        P(COL, None),
    )
    out_specs = P("tm", COL, None)
    return jax.shard_map(body, mesh=torus, in_specs=in_specs, out_specs=out_specs, check_vma=False)
```

```python
import functools

import jax
import jax.numpy as jnp
from jax import lax
from jax.experimental import pallas as pl
from jax.experimental.pallas import tpu as pltpu
from jax.sharding import Mesh
from jax.sharding import PartitionSpec as P

COL = ("zh", "zl", "xl")
ALL = ("tm",) + COL
F32, BF16 = jnp.float32, jnp.bfloat16
FEW = pl.BlockSpec(memory_space=pltpu.SMEM)
WHOLE = pl.BlockSpec(memory_space=pltpu.VMEM)
SMALL, LARGE = 12 << 20, 20 << 20
BLOCK = 4
PICKCOST = 1 << 35
FIRST = 2


def far_ref(value):
    return pltpu.with_memory_space_constraint(value, pltpu.HBM)


def pick_kernel(
    share,
    times_hbm,
    occ_energy_hbm,
    emp_energy_hbm,
    occ_hbm,
    emp_hbm,
    out_ref,
    factor_ref,
    held,
    times_ref,
    energy_ref,
    sems,
):
    team = lax.axis_index("tm")
    shares = team, jnp.where(team & 1 == 1, team ^ 2, team)
    pairs = []
    for side in range(2):
        near = pl.multiple_of(shares[side] * share // 8 * 8, 8)
        for kind, ref in enumerate((occ_hbm, emp_hbm)):
            pairs.append((ref.at[pl.ds(near, 8)], held.at[2 * side + kind]))
    pairs.append((times_hbm, times_ref))
    pairs.append((occ_energy_hbm, energy_ref.at[0]))
    pairs.append((emp_energy_hbm, energy_ref.at[1]))
    copies = [pltpu.make_async_copy(*pair, sems.at[i]) for i, pair in enumerate(pairs)]
    for copy in copies:
        copy.start()
    line = lax.broadcasted_iota(jnp.int32, (2 * share, 8), 0)
    point = lax.broadcasted_iota(jnp.int32, (2 * share, 8), 1)
    for side in range(2):
        first = lax.rem(shares[side] * share, 8)
        occ_pick = jnp.where((line < share) & (point == first + line), 1.0, 0.0).astype(BF16)
        emp_pick = jnp.where((line >= share) & (point == first + line - share), 1.0, 0.0)
        copies[2 * side].wait()
        copies[2 * side + 1].wait()
        both = jnp.dot(occ_pick, held[2 * side], preferred_element_type=F32)
        both += jnp.dot(emp_pick.astype(BF16), held[2 * side + 1], preferred_element_type=F32)
        both = both.astype(BF16)
        for peer in range(side, out_ref.shape[0], 2):
            out_ref[peer] = both
    for copy in copies[4:7]:
        copy.wait()
    times = times_ref.shape[1]
    row = lax.broadcasted_iota(jnp.int32, (times, times), 0)
    lane = lax.broadcasted_iota(jnp.int32, (times, times), 1)
    moments = jnp.sum(jnp.where(row == lane, times_ref[...], 0.0), axis=1, keepdims=True)
    for kind in range(2):
        factor_ref[kind] = jnp.exp(-energy_ref[kind] * moments)


def pick(times, occ_energy, emp_energy, occ_t, emp_t, peers, share):
    states = occ_t.shape[1]
    far = pl.BlockSpec(memory_space=pltpu.HBM)
    count = times.shape[0]
    return pl.pallas_call(
        functools.partial(pick_kernel, share),
        out_shape=(
            jax.ShapeDtypeStruct((peers, 2 * share, states), BF16),
            jax.ShapeDtypeStruct((2, count, states), F32),
        ),
        in_specs=[far] * 5,
        out_specs=(WHOLE,) * 2,
        scratch_shapes=[
            pltpu.VMEM((4, 8, states), BF16),
            pltpu.VMEM((1, count), F32),
            pltpu.VMEM((2, 1, states), F32),
            pltpu.SemaphoreType.DMA((7,)),
        ],
        compiler_params=pltpu.CompilerParams(vmem_limit_bytes=SMALL),
        cost_estimate=pl.CostEstimate(flops=PICKCOST, bytes_accessed=1 << 20, transcendentals=0),
    )(
        far_ref(times[None, :]),
        far_ref(occ_energy[None, :]),
        far_ref(emp_energy[None, :]),
        far_ref(occ_t),
        far_ref(emp_t),
    )


def halves(value):
    high = value.astype(BF16)
    return high, (value - high.astype(F32)).astype(BF16)


def scale(share, part, rows_ref, factor_ref, scaled):
    times = factor_ref.shape[1]
    occ_s, emp_s = scaled
    start = 2 * (lax.axis_index("zl") ^ (part >> 1)) + (lax.axis_index("xl") ^ (part & 1))
    for index in range(BLOCK):
        rows = rows_ref[4 * index + start].astype(F32)
        for r in range(share):
            at = (index * share + r) * times
            occ_s[at : at + times, :] = (rows[r : r + 1, :] * factor_ref[0]).astype(BF16)
            emp_s[at : at + times, :] = (
                rows[share + r : share + r + 1, :] * factor_ref[1]
            ).astype(BF16)


def first_kernel(
    share,
    part,
    rows_ref,
    factor_ref,
    occ_ref,
    emp_ref,
    trial_ref,
    out_ref,
    high_ref,
    low_ref,
    *scaled,
):
    for begin in range(0, trial_ref.shape[0], 256):
        at = slice(begin, begin + 256)
        high_ref[at, :], low_ref[at, :] = halves(trial_ref[at, :])
    next_kernel(
        share, part, rows_ref, factor_ref, occ_ref, emp_ref, high_ref, low_ref, out_ref, *scaled
    )


def next_kernel(
    share, part, rows_ref, factor_ref, occ_ref, emp_ref, high_ref, low_ref, out_ref, *scaled
):
    scale(share, part, rows_ref, factor_ref, scaled)
    polar = jnp.dot(scaled[0][...], occ_ref[...], preferred_element_type=F32)
    polar *= jnp.dot(scaled[1][...], emp_ref[...], preferred_element_type=F32)
    polar = polar.astype(BF16)
    total = jnp.dot(polar, high_ref[...], preferred_element_type=F32)
    total += jnp.dot(polar, low_ref[...], preferred_element_type=F32)
    out_ref[...] = total.astype(out_ref.dtype)


def table_kernel(share, part, times_ref, weights_ref, freqs_ref, *refs):
    times, freqs = times_ref.shape[0], freqs_ref.shape[0]
    points = BLOCK * share
    lines = points * times
    line = lax.broadcasted_iota(jnp.int32, (freqs, lines), 0)
    lane = lax.broadcasted_iota(jnp.int32, (freqs, lines), 1)
    moment, weight, freq = (jnp.zeros((freqs, lines), F32) for _ in range(3))
    for t in range(times):
        moment = jnp.where(lane % times == t, times_ref[t], moment)
        weight = jnp.where(lane % times == t, weights_ref[t], weight)
    for k in range(freqs):
        freq = jnp.where(line == k, freqs_ref[k], freq)
    table = weight * jnp.cos(freq * moment)
    point = lax.broadcasted_iota(jnp.int32, (points, lines), 0)
    same = lax.broadcasted_iota(jnp.int32, (points, lines), 1) // times == point
    *inputs, out_ref, spread_ref, occ_s, emp_s = refs
    for k in range(freqs):
        main, rest = halves(jnp.where(same, table[k : k + 1, :], 0.0))
        spread_ref[0, k * points : (k + 1) * points, :] = main
        spread_ref[1, k * points : (k + 1) * points, :] = rest
    next_kernel(share, part, *inputs, out_ref, occ_s, emp_s)


def cost(lines, states, columns, trials):
    return pl.CostEstimate(
        flops=4 * lines * columns * (states + trials), bytes_accessed=8 << 20, transcendentals=0
    )


def first_products(part, rows, factor, occ_cols, emp_cols, trial, share):
    states, columns = occ_cols.shape
    lines, trials = BLOCK * share * factor.shape[1], trial.shape[1]
    return pl.pallas_call(
        functools.partial(first_kernel, share, part),
        out_shape=(
            jax.ShapeDtypeStruct((lines, trials), BF16),
            jax.ShapeDtypeStruct(trial.shape, BF16),
            jax.ShapeDtypeStruct(trial.shape, BF16),
        ),
        in_specs=[WHOLE] * 5,
        out_specs=(WHOLE,) * 3,
        scratch_shapes=[pltpu.VMEM((lines, states), BF16)] * 2,
        compiler_params=pltpu.CompilerParams(vmem_limit_bytes=LARGE),
        cost_estimate=cost(lines, states, columns, trials),
    )(rows, factor, occ_cols, emp_cols, trial)


def next_products(part, rows, factor, occ_cols, emp_cols, high, low, share, dtype, grid=None):
    times, states = factor.shape[1:]
    columns, trials = high.shape
    lines = BLOCK * share * times
    out = jax.ShapeDtypeStruct((lines, trials), dtype)
    grid = () if grid is None else grid
    return pl.pallas_call(
        functools.partial(table_kernel if grid else next_kernel, share, part),
        out_shape=(out, jax.ShapeDtypeStruct((2, lines, lines), BF16)) if grid else out,
        in_specs=[FEW] * len(grid) + [WHOLE] * 6,
        out_specs=(WHOLE, WHOLE) if grid else WHOLE,
        scratch_shapes=[pltpu.VMEM((lines, states), BF16)] * 2,
        compiler_params=pltpu.CompilerParams(vmem_limit_bytes=LARGE),
        cost_estimate=cost(lines, states, columns, trials),
    )(*grid, rows, factor, occ_cols, emp_cols, high, low)


def last_order(members, zs):
    teams = range(members // zs)
    return [t * zs + z for z in range(zs)[::-1] for t in teams[::-1]]


def mix_kernel(share, spread_ref, own_ref, *refs):
    *parts, out_ref = refs
    total = own_ref[...]
    for part in parts:
        total += part[...].astype(F32)
    main, rest = halves(total)
    mixed = jnp.dot(spread_ref[0], rest, preferred_element_type=F32)
    mixed += jnp.dot(spread_ref[1], main, preferred_element_type=F32)
    mixed += jnp.dot(spread_ref[0], main, preferred_element_type=F32)
    mixed = mixed.astype(BF16)
    for place, member in enumerate(last_order(out_ref.shape[0], BLOCK)):
        out_ref[place] = mixed[member * share : (member + 1) * share, :]


def mix(spread, own, *rest):
    *parts, share = rest
    lines, trials = own.shape
    return pl.pallas_call(
        functools.partial(mix_kernel, share),
        out_shape=jax.ShapeDtypeStruct((lines // share, share, trials), BF16),
        in_specs=[WHOLE] * (2 + len(parts)),
        out_specs=WHOLE,
        compiler_params=pltpu.CompilerParams(vmem_limit_bytes=SMALL),
    )(spread, own, *parts)


def collect_kernel(teams, got_ref, out_ref):
    share = got_ref.shape[1]
    zs = got_ref.shape[0] // teams
    turn = lax.axis_index("xl")
    order = last_order(got_ref.shape[0], zs)
    for place in range(teams):
        total = None
        for z in range(zs):
            slot = order.index(place * zs + z)
            if place & 1:
                slot = jnp.where(turn == 0, slot, order.index((place ^ 2) * zs + z))
            part = got_ref[slot].astype(F32)
            total = part if total is None else total + part
        out_ref[0, place * share : (place + 1) * share, :] = total


def collect(got, teams):
    share, trials = got.shape[1:]
    return pl.pallas_call(
        functools.partial(collect_kernel, teams),
        out_shape=jax.ShapeDtypeStruct((1, teams * share, trials), F32),
        in_specs=[WHOLE],
        out_specs=WHOLE,
        compiler_params=pltpu.CompilerParams(vmem_limit_bytes=SMALL),
    )(got)


def pairs_of(teams, zs, along_x, along_z):
    pairs = []
    for tm in range(teams):
        for z in range(zs):
            for xl in range(2):
                team, to = tm, z
                if along_x and tm & 1:
                    team = tm ^ 2
                if along_z:
                    to = (z - 1 + 2 * (z & 1)) % zs if tm & 1 else z ^ 1
                pairs.append(((tm * zs + z) * 2 + xl, (team * zs + to) * 2 + (xl ^ along_x)))
    return pairs


def body(
    occ_rows,
    emp_rows,
    occ_cols,
    emp_cols,
    occ_energy,
    emp_energy,
    time_points,
    time_weights,
    frequencies,
    trial_vectors,
):
    teams, zs = lax.axis_size("tm"), 2 * lax.axis_size("zh")
    share = occ_rows.shape[1] // teams

    sent, factor = pick(
        time_points,
        occ_energy,
        emp_energy,
        occ_rows.T,
        emp_rows.T,
        2 * zs,
        share,
    )
    rows = lax.all_to_all(sent, COL, split_axis=0, concat_axis=0, tiled=True)

    both, high, low = first_products(3, rows, factor, occ_cols, emp_cols, trial_vectors, share)
    held = (rows, factor, occ_cols, emp_cols, high, low, share)
    from_both = lax.ppermute(both, ALL, pairs_of(teams, zs, 1, 1))
    first = next_products(FIRST, *held, BF16)
    from_first = lax.ppermute(first, ALL, pairs_of(teams, zs, FIRST & 1, FIRST >> 1))
    second = next_products(3 - FIRST, *held, BF16)
    from_second = lax.ppermute(second, ALL, pairs_of(teams, zs, 1 - (FIRST & 1), 1 - (FIRST >> 1)))
    grid = tuple(map(far_ref, (time_points, time_weights, frequencies)))
    own, spread = next_products(0, *held, F32, grid)
    sent = mix(spread, own, from_both, from_first, from_second, share)
    got = lax.all_to_all(
        sent,
        ("tm", "zh"),
        split_axis=0,
        concat_axis=0,
        axis_index_groups=[last_order(sent.shape[0], zs // 2)],
        tiled=True,
    )
    return collect(got, teams)


def solution(mesh):
    torus = Mesh(mesh.devices.reshape(mesh.shape["tm"], mesh.shape["col"] // 4, 2, 2), ALL)
    in_specs = (
        P(None, COL),
        P(None, COL),
        P(None, COL),
        P(None, COL),
        P(),
        P(),
        P(),
        P(),
        P(),
        P(COL, None),
    )
    out_specs = P("tm", COL, None)
    return jax.shard_map(body, mesh=torus, in_specs=in_specs, out_specs=out_specs, check_vma=False)
```

```python
import functools

import jax
import jax.numpy as jnp
from jax import lax
from jax.experimental import pallas as pl
from jax.experimental.pallas import tpu as pltpu
from jax.sharding import Mesh
from jax.sharding import PartitionSpec as P

COL = ("zh", "zl", "xl")
ALL = ("tm",) + COL
F32, BF16 = jnp.float32, jnp.bfloat16
FEW = pl.BlockSpec(memory_space=pltpu.SMEM)
WHOLE = pl.BlockSpec(memory_space=pltpu.VMEM)
SMALL, LARGE = 12 << 20, 20 << 20
BLOCK = 4
PICKCOST = 1 << 35
FIRST = 2


def far_ref(value):
    return pltpu.with_memory_space_constraint(value, pltpu.HBM)


def ring_order(peers):
    zs = range(peers // 2)
    return [2 * (-z % len(zs)) + xl for xl in range(2) for z in zs]


def pick_kernel(
    share,
    times_hbm,
    occ_energy_hbm,
    emp_energy_hbm,
    occ_hbm,
    emp_hbm,
    out_ref,
    factor_ref,
    held,
    times_ref,
    energy_ref,
    sems,
):
    team = lax.axis_index("tm")
    shares = team, jnp.where(team & 1 == 1, team ^ 2, team)
    pairs = []
    for side in range(2):
        near = pl.multiple_of(shares[side] * share // 8 * 8, 8)
        for kind, ref in enumerate((occ_hbm, emp_hbm)):
            pairs.append((ref.at[pl.ds(near, 8)], held.at[2 * side + kind]))
    pairs.append((times_hbm, times_ref))
    pairs.append((occ_energy_hbm, energy_ref.at[0]))
    pairs.append((emp_energy_hbm, energy_ref.at[1]))
    copies = [pltpu.make_async_copy(*pair, sems.at[i]) for i, pair in enumerate(pairs)]
    for copy in copies:
        copy.start()
    line = lax.broadcasted_iota(jnp.int32, (2 * share, 8), 0)
    point = lax.broadcasted_iota(jnp.int32, (2 * share, 8), 1)
    for side in range(2):
        first = lax.rem(shares[side] * share, 8)
        occ_pick = jnp.where((line < share) & (point == first + line), 1.0, 0.0).astype(BF16)
        emp_pick = jnp.where((line >= share) & (point == first + line - share), 1.0, 0.0)
        copies[2 * side].wait()
        copies[2 * side + 1].wait()
        both = jnp.dot(occ_pick, held[2 * side], preferred_element_type=F32)
        both += jnp.dot(emp_pick.astype(BF16), held[2 * side + 1], preferred_element_type=F32)
        both = both.astype(BF16)
        for place, peer in enumerate(ring_order(out_ref.shape[0])):
            if peer % 2 == side:
                out_ref[place] = both
    for copy in copies[4:7]:
        copy.wait()
    times = times_ref.shape[1]
    row = lax.broadcasted_iota(jnp.int32, (times, times), 0)
    lane = lax.broadcasted_iota(jnp.int32, (times, times), 1)
    moments = jnp.sum(jnp.where(row == lane, times_ref[...], 0.0), axis=1, keepdims=True)
    for kind in range(2):
        factor_ref[kind] = jnp.exp(-energy_ref[kind] * moments)


def pick(times, occ_energy, emp_energy, occ_t, emp_t, peers, share):
    states = occ_t.shape[1]
    far = pl.BlockSpec(memory_space=pltpu.HBM)
    count = times.shape[0]
    return pl.pallas_call(
        functools.partial(pick_kernel, share),
        out_shape=(
            jax.ShapeDtypeStruct((peers, 2 * share, states), BF16),
            jax.ShapeDtypeStruct((2, count, states), F32),
        ),
        in_specs=[far] * 5,
        out_specs=(WHOLE,) * 2,
        scratch_shapes=[
            pltpu.VMEM((4, 8, states), BF16),
            pltpu.VMEM((1, count), F32),
            pltpu.VMEM((2, 1, states), F32),
            pltpu.SemaphoreType.DMA((7,)),
        ],
        compiler_params=pltpu.CompilerParams(vmem_limit_bytes=SMALL),
        cost_estimate=pl.CostEstimate(flops=PICKCOST, bytes_accessed=1 << 20, transcendentals=0),
    )(
        far_ref(times[None, :]),
        far_ref(occ_energy[None, :]),
        far_ref(emp_energy[None, :]),
        far_ref(occ_t),
        far_ref(emp_t),
    )


def halves(value):
    high = value.astype(BF16)
    return high, (value - high.astype(F32)).astype(BF16)


def scale(share, part, rows_ref, factor_ref, scaled):
    times = factor_ref.shape[1]
    occ_s, emp_s = scaled
    kind = 2 * (lax.axis_index("zl") ^ (part >> 1)) + (lax.axis_index("xl") ^ (part & 1))
    order = ring_order(rows_ref.shape[0])
    for index in range(BLOCK):
        slot = order.index(4 * index)
        for other in range(1, 4):
            slot = jnp.where(kind == other, order.index(4 * index + other), slot)
        rows = rows_ref[slot].astype(F32)
        for r in range(share):
            at = (index * share + r) * times
            occ_s[at : at + times, :] = (rows[r : r + 1, :] * factor_ref[0]).astype(BF16)
            emp_s[at : at + times, :] = (
                rows[share + r : share + r + 1, :] * factor_ref[1]
            ).astype(BF16)


def first_kernel(
    share,
    part,
    rows_ref,
    factor_ref,
    occ_ref,
    emp_ref,
    trial_ref,
    out_ref,
    high_ref,
    low_ref,
    *scaled,
):
    for begin in range(0, trial_ref.shape[0], 256):
        at = slice(begin, begin + 256)
        high_ref[at, :], low_ref[at, :] = halves(trial_ref[at, :])
    next_kernel(
        share, part, rows_ref, factor_ref, occ_ref, emp_ref, high_ref, low_ref, out_ref, *scaled
    )


def next_kernel(
    share, part, rows_ref, factor_ref, occ_ref, emp_ref, high_ref, low_ref, out_ref, *scaled
):
    scale(share, part, rows_ref, factor_ref, scaled)
    polar = jnp.dot(scaled[0][...], occ_ref[...], preferred_element_type=F32)
    polar *= jnp.dot(scaled[1][...], emp_ref[...], preferred_element_type=F32)
    polar = polar.astype(BF16)
    total = jnp.dot(polar, high_ref[...], preferred_element_type=F32)
    total += jnp.dot(polar, low_ref[...], preferred_element_type=F32)
    out_ref[...] = total.astype(out_ref.dtype)


def table_kernel(share, part, times_ref, weights_ref, freqs_ref, *refs):
    times, freqs = times_ref.shape[0], freqs_ref.shape[0]
    points = BLOCK * share
    lines = points * times
    line = lax.broadcasted_iota(jnp.int32, (freqs, lines), 0)
    lane = lax.broadcasted_iota(jnp.int32, (freqs, lines), 1)
    moment, weight, freq = (jnp.zeros((freqs, lines), F32) for _ in range(3))
    for t in range(times):
        moment = jnp.where(lane % times == t, times_ref[t], moment)
        weight = jnp.where(lane % times == t, weights_ref[t], weight)
    for k in range(freqs):
        freq = jnp.where(line == k, freqs_ref[k], freq)
    table = weight * jnp.cos(freq * moment)
    point = lax.broadcasted_iota(jnp.int32, (points, lines), 0)
    same = lax.broadcasted_iota(jnp.int32, (points, lines), 1) // times == point
    *inputs, out_ref, spread_ref, occ_s, emp_s = refs
    for k in range(freqs):
        main, rest = halves(jnp.where(same, table[k : k + 1, :], 0.0))
        spread_ref[0, k * points : (k + 1) * points, :] = main
        spread_ref[1, k * points : (k + 1) * points, :] = rest
    next_kernel(share, part, *inputs, out_ref, occ_s, emp_s)


def cost(lines, states, columns, trials):
    return pl.CostEstimate(
        flops=4 * lines * columns * (states + trials), bytes_accessed=8 << 20, transcendentals=0
    )


def first_products(part, rows, factor, occ_cols, emp_cols, trial, share):
    states, columns = occ_cols.shape
    lines, trials = BLOCK * share * factor.shape[1], trial.shape[1]
    return pl.pallas_call(
        functools.partial(first_kernel, share, part),
        out_shape=(
            jax.ShapeDtypeStruct((lines, trials), BF16),
            jax.ShapeDtypeStruct(trial.shape, BF16),
            jax.ShapeDtypeStruct(trial.shape, BF16),
        ),
        in_specs=[WHOLE] * 5,
        out_specs=(WHOLE,) * 3,
        scratch_shapes=[pltpu.VMEM((lines, states), BF16)] * 2,
        compiler_params=pltpu.CompilerParams(vmem_limit_bytes=LARGE),
        cost_estimate=cost(lines, states, columns, trials),
    )(rows, factor, occ_cols, emp_cols, trial)


def next_products(part, rows, factor, occ_cols, emp_cols, high, low, share, dtype, grid=None):
    times, states = factor.shape[1:]
    columns, trials = high.shape
    lines = BLOCK * share * times
    out = jax.ShapeDtypeStruct((lines, trials), dtype)
    grid = () if grid is None else grid
    return pl.pallas_call(
        functools.partial(table_kernel if grid else next_kernel, share, part),
        out_shape=(out, jax.ShapeDtypeStruct((2, lines, lines), BF16)) if grid else out,
        in_specs=[FEW] * len(grid) + [WHOLE] * 6,
        out_specs=(WHOLE, WHOLE) if grid else WHOLE,
        scratch_shapes=[pltpu.VMEM((lines, states), BF16)] * 2,
        compiler_params=pltpu.CompilerParams(vmem_limit_bytes=LARGE),
        cost_estimate=cost(lines, states, columns, trials),
    )(*grid, rows, factor, occ_cols, emp_cols, high, low)


def last_order(members, zs):
    teams = range(members // zs)
    return [t * zs + z for t in teams[::-1] for z in range(zs)[::-1]]


def mix_kernel(share, spread_ref, own_ref, *refs):
    *parts, out_ref = refs
    total = own_ref[...]
    for part in parts:
        total += part[...].astype(F32)
    main, rest = halves(total)
    mixed = jnp.dot(spread_ref[0], rest, preferred_element_type=F32)
    mixed += jnp.dot(spread_ref[1], main, preferred_element_type=F32)
    mixed += jnp.dot(spread_ref[0], main, preferred_element_type=F32)
    mixed = mixed.astype(BF16)
    for place, member in enumerate(last_order(out_ref.shape[0], BLOCK)):
        out_ref[place] = mixed[member * share : (member + 1) * share, :]


def mix(spread, own, *rest):
    *parts, share = rest
    lines, trials = own.shape
    return pl.pallas_call(
        functools.partial(mix_kernel, share),
        out_shape=jax.ShapeDtypeStruct((lines // share, share, trials), BF16),
        in_specs=[WHOLE] * (2 + len(parts)),
        out_specs=WHOLE,
        compiler_params=pltpu.CompilerParams(vmem_limit_bytes=SMALL),
    )(spread, own, *parts)


def collect_kernel(teams, got_ref, out_ref):
    share = got_ref.shape[1]
    zs = got_ref.shape[0] // teams
    turn = lax.axis_index("xl")
    order = last_order(got_ref.shape[0], zs)
    for place in range(teams):
        total = None
        for z in range(zs):
            slot = order.index(place * zs + z)
            if place & 1:
                slot = jnp.where(turn == 0, slot, order.index((place ^ 2) * zs + z))
            part = got_ref[slot].astype(F32)
            total = part if total is None else total + part
        out_ref[0, place * share : (place + 1) * share, :] = total


def collect(got, teams):
    share, trials = got.shape[1:]
    return pl.pallas_call(
        functools.partial(collect_kernel, teams),
        out_shape=jax.ShapeDtypeStruct((1, teams * share, trials), F32),
        in_specs=[WHOLE],
        out_specs=WHOLE,
        compiler_params=pltpu.CompilerParams(vmem_limit_bytes=SMALL),
    )(got)


def pairs_of(teams, zs, along_x, along_z):
    pairs = []
    for tm in range(teams):
        for z in range(zs):
            for xl in range(2):
                team, to = tm, z
                if along_x and tm & 1:
                    team = tm ^ 2
                if along_z:
                    to = (z - 1 + 2 * (z & 1)) % zs if tm & 1 else z ^ 1
                pairs.append(((tm * zs + z) * 2 + xl, (team * zs + to) * 2 + (xl ^ along_x)))
    return pairs


def body(
    occ_rows,
    emp_rows,
    occ_cols,
    emp_cols,
    occ_energy,
    emp_energy,
    time_points,
    time_weights,
    frequencies,
    trial_vectors,
):
    teams, zs = lax.axis_size("tm"), 2 * lax.axis_size("zh")
    share = occ_rows.shape[1] // teams

    sent, factor = pick(
        time_points,
        occ_energy,
        emp_energy,
        occ_rows.T,
        emp_rows.T,
        2 * zs,
        share,
    )
    rows = lax.all_to_all(
        sent,
        COL,
        split_axis=0,
        concat_axis=0,
        axis_index_groups=[ring_order(2 * zs)],
        tiled=True,
    )

    both, high, low = first_products(3, rows, factor, occ_cols, emp_cols, trial_vectors, share)
    held = (rows, factor, occ_cols, emp_cols, high, low, share)
    from_both = lax.ppermute(both, ALL, pairs_of(teams, zs, 1, 1))
    first = next_products(FIRST, *held, BF16)
    from_first = lax.ppermute(first, ALL, pairs_of(teams, zs, FIRST & 1, FIRST >> 1))
    second = next_products(3 - FIRST, *held, BF16)
    from_second = lax.ppermute(second, ALL, pairs_of(teams, zs, 1 - (FIRST & 1), 1 - (FIRST >> 1)))
    grid = tuple(map(far_ref, (time_points, time_weights, frequencies)))
    own, spread = next_products(0, *held, F32, grid)
    sent = mix(spread, own, from_both, from_first, from_second, share)
    got = lax.all_to_all(
        sent,
        ("tm", "zh"),
        split_axis=0,
        concat_axis=0,
        axis_index_groups=[last_order(sent.shape[0], zs // 2)],
        tiled=True,
    )
    return collect(got, teams)


def solution(mesh):
    torus = Mesh(mesh.devices.reshape(mesh.shape["tm"], mesh.shape["col"] // 4, 2, 2), ALL)
    in_specs = (
        P(None, COL),
        P(None, COL),
        P(None, COL),
        P(None, COL),
        P(),
        P(),
        P(),
        P(),
        P(),
        P(COL, None),
    )
    out_specs = P("tm", COL, None)
    return jax.shard_map(body, mesh=torus, in_specs=in_specs, out_specs=out_specs, check_vma=False)
```
